768 devices in a mesh: replica: 48 (over x_lo, z, core), fsdp: 16 (over y, x_hi).
Axes of the slice: x: 4 (x_hi: 2, x_lo: 2; x = x_hi * 2 + x_lo), y: 8, z: 12, core: 2. Of those that a mesh axis runs over, the one named last changes fastest.
Arguments:
- tokens: bfloat16 [98304, 8192], P(('replica', 'fsdp')), may hold values from -6 to 6
- target: bfloat16 [98304, 512], P(('replica', 'fsdp')), may hold values from -6 to 6
- weight: bfloat16 [48, 8192, 512], P('replica', 'fsdp'), may hold values from -6 to 6
- pseudo: float32 [48, 8192, 512], P('replica', 'fsdp'), may hold values from -6 to 6
- global_frag: float32 [8192, 512], P('fsdp'), may hold values from -6 to 6
- momentum: float32 [8192, 512], P('fsdp'), may hold values from -2 to 2
Outputs:
- new_weight: bfloat16 [48, 8192, 512], P('replica', 'fsdp')
- residual: bfloat16 [98304, 512], P(('replica', 'fsdp'))
- new_global: float32 [8192, 512], P('fsdp')
- new_momentum: float32 [8192, 512], P('fsdp')
The draws below stay inside these ranges and needn't reach their ends.
All inputs are finite; a program needn't handle non-finite values.
Results may differ from the reference program's by a relative error of at most 0.013.
Values may be sent and summed in bfloat16 or wider, within the bound.
No kernel may reach another device: no remote copies, remote signals or barrier semaphores. Data moves between devices by JAX's collectives and lax.ppermute only.
A program may use at most 64 MiB of HBM per device.

```python
import jax
import jax.numpy as jnp
from jax import lax

D = 8192
KV = 512
TOK_DEV = 128
TOK_ALL = 98304
N_REPLICA = 48
N_FSDP = 16


def level_of(rng, extent, cuts, smallest, high):
    def one(position, shards_of):
        draws = jax.random.uniform(jax.random.fold_in(jax.random.fold_in(rng, 6), position), (shards_of,), jnp.float32, smallest / len(cuts), high / len(cuts))
        return jnp.repeat(jnp.exp(draws), extent[position] // shards_of).reshape((-1,) + (1,) * (len(extent) - position - 1))

    gain = one(*cuts[0])
    for cut in cuts[1:]:
        gain = gain * one(*cut)
    return gain


def scatter_about(own_key, extent, width, bound, pieces=(), kind=jnp.bfloat16):
    array = width * jax.random.normal(own_key, extent, jnp.float32)
    if pieces:
        array = array * level_of(own_key, extent, pieces, -0.22, 0.18)
    return jnp.clip(array, -bound, bound).astype(kind)


def setup_inputs(seed: int = 0) -> dict:
    seeds = jax.random.split(jax.random.key(seed), 7)
    return {
        "tokens": scatter_about(seeds[0], (TOK_ALL, D), 1.0, 6.0, ((0, 768),)),
        "target": scatter_about(seeds[1], (TOK_ALL, KV), 1.0, 6.0, ((0, 768),)),
        "weight": scatter_about(seeds[2], (N_REPLICA, D, KV), 1.0, 6.0, ((0, 48), (1, 16))),
        "pseudo": scatter_about(seeds[3], (N_REPLICA, D, KV), 1.0, 6.0, ((0, 48), (1, 16)), jnp.float32),
        "global_frag": scatter_about(seeds[4], (D, KV), 1.0, 6.0, ((0, 16),), jnp.float32),
        "momentum": scatter_about(seeds[5], (D, KV), 0.3, 2.0, ((0, 16),), jnp.float32),
    }


inner_rate = 1.0
outer_rate = 0.7
nesterov_coef = 0.9
merge_share = 0.5


def reference(tokens, target, weight, pseudo, global_frag, momentum):
    key_scale = D ** -0.5
    replica_rows = TOK_DEV * N_FSDP
    block_width = D // N_FSDP

    def replica_step(operands):
        inputs_rep, target_rep, weight_rep = operands
        token_blocks = inputs_rep.reshape(replica_rows, N_FSDP, block_width).astype(jnp.float32)
        weight_blocks = weight_rep.reshape(N_FSDP, block_width, KV).astype(jnp.float32)
        partials = jnp.einsum('tfd,fdk->ftk', token_blocks, weight_blocks) * key_scale
        rounded = lax.optimization_barrier(partials.astype(jnp.bfloat16))
        keys = jnp.sum(rounded.astype(jnp.float32), axis=0)
        residual_rep = (keys - target_rep.astype(jnp.float32)).astype(jnp.bfloat16)
        gradient = lax.dot_general(inputs_rep, residual_rep, (((0,), (0,)), ((), ())),
                                   preferred_element_type=jnp.float32) * key_scale
        stepped = weight_rep.astype(jnp.float32) - inner_rate * gradient
        return stepped, residual_rep

    inputs_all = tokens.reshape(N_REPLICA, replica_rows, D)
    targets_all = target.reshape(N_REPLICA, replica_rows, KV)
    stepped, residual_all = lax.map(replica_step, (inputs_all, targets_all, weight))
    averaged = jnp.sum(pseudo, axis=0) / N_REPLICA
    new_momentum = nesterov_coef * momentum + averaged
    new_global = global_frag - outer_rate * (averaged + nesterov_coef * new_momentum)
    new_weight = (merge_share * stepped + (1.0 - merge_share) * new_global[None]).astype(jnp.bfloat16)
    return new_weight, residual_all.reshape(N_REPLICA * replica_rows, KV), new_global, new_momentum
```

```python
import functools

import jax
import jax.numpy as jnp
from jax import lax
from jax.experimental import pallas as pl
from jax.experimental.pallas import tpu as pltpu
from jax.sharding import Mesh
from jax.sharding import PartitionSpec as P


Y = ("yh", "yl")
FSDP = ("yh", "yl", "xh")
REPLICA = ("xl", "zh", "zl", "core")
SWAP = [(0, 1), (1, 0)]
VMEM_LIMIT = 16 * 2**20

inner_rate = 1.0
outer_rate = 0.7
nesterov_coef = 0.9
merge_share = 0.5


def halved(total, axis, dim):
    me = lax.axis_index(axis)
    sent = lax.dynamic_index_in_dim(total, 1 - me, dim, keepdims=False).astype(jnp.bfloat16)
    got = lax.ppermute(sent, axis, SWAP)
    return lax.dynamic_index_in_dim(total, me, dim, keepdims=False) + got.astype(jnp.float32)


def replica_mean(pseudo):
    rows, columns = pseudo.shape
    replicas = lax.axis_size(REPLICA)
    total = pseudo.reshape(2, 2, 2, rows // 8, columns)
    total = halved(total, "core", 2)
    total = halved(total, "xl", 0)
    total = halved(total, "zl", 0)
    parts = lax.all_gather(total.astype(jnp.bfloat16), "zh", axis=0)
    mean = (jnp.sum(parts.astype(jnp.float32), axis=0) / replicas).astype(jnp.bfloat16)
    return lax.all_gather(mean, ("xl", "zl", "core"), axis=0, tiled=True).astype(jnp.float32)


def split_kernel(tokens_ref, out_ref):
    out_ref[0] = tokens_ref[...]


def split_columns(tokens, parts):
    rows, columns = tokens.shape
    width = columns // parts
    return pl.pallas_call(
        split_kernel,
        grid=(parts,),
        in_specs=[pl.BlockSpec((rows, width), lambda i: (0, i))],
        out_specs=pl.BlockSpec((1, rows, width), lambda i: (i, 0, 0)),
        out_shape=jax.ShapeDtypeStruct((parts, rows, width), tokens.dtype),
        name="split_columns",
    )(tokens)


def partial_kernel(scale, place_ref, x_ref, own_ref, other_ref, out_ref):
    width = own_ref.shape[0]
    low, high = x_ref[0, :, :width], x_ref[0, :, width:]

    def emit(low_rows, high_rows):
        total = jnp.dot(low, low_rows[...], preferred_element_type=jnp.float32)
        total += jnp.dot(high, high_rows[...], preferred_element_type=jnp.float32)
        out_ref[0] = (total * scale).astype(out_ref.dtype)

    @pl.when(place_ref[1] == 0)
    def _():
        emit(own_ref, other_ref)

    @pl.when(place_ref[1] != 0)
    def _():
        emit(other_ref, own_ref)


def partial_keys(place, blocks, own_rows, other_rows, scale):
    parts, rows, columns = blocks.shape
    width, key_width = own_rows.shape
    whole = pl.BlockSpec((width, key_width), lambda i, place: (0, 0))
    return pl.pallas_call(
        functools.partial(partial_kernel, scale),
        grid_spec=pltpu.PrefetchScalarGridSpec(
            num_scalar_prefetch=1,
            grid=(parts,),
            in_specs=[pl.BlockSpec((1, rows, columns), lambda i, place: (i, 0, 0)), whole, whole],
            out_specs=pl.BlockSpec((1, rows, key_width), lambda i, place: (i, 0, 0)),
        ),
        out_shape=jax.ShapeDtypeStruct((parts, rows, key_width), jnp.bfloat16),
        cost_estimate=pl.CostEstimate(
            flops=2 * parts * rows * columns * key_width,
            bytes_accessed=2 * parts * rows * (columns + key_width) + 4 * width * key_width,
            transcendentals=0,
        ),
        compiler_params=pltpu.CompilerParams(vmem_limit_bytes=VMEM_LIMIT),
        name="partial_keys",
    )(place, blocks, own_rows, other_rows)


def turn_kernel(place_ref, near_ref, far_ref, send_near, keep_near, send_far, keep_far):
    width = send_near.shape[0]

    def emit(keep, send):
        for source, kept, sent in ((near_ref, keep_near, send_near), (far_ref, keep_far, send_far)):
            kept[...] = source[0, :, keep * width : (keep + 1) * width].T
            sent[...] = source[0, :, send * width : (send + 1) * width].T

    @pl.when(place_ref[1] == 0)
    def _():
        emit(0, 1)

    @pl.when(place_ref[1] != 0)
    def _():
        emit(1, 0)


def turned(place, blocks):
    parts, rows, columns = blocks.shape
    width = columns // 2
    out = jax.ShapeDtypeStruct((width, parts // 2 * rows), blocks.dtype)
    return pl.pallas_call(
        turn_kernel,
        grid_spec=pltpu.PrefetchScalarGridSpec(
            num_scalar_prefetch=1,
            grid=(parts // 2,),
            in_specs=[
                pl.BlockSpec((1, rows, columns), lambda k, place: (2 * k + place[0], 0, 0)),
                pl.BlockSpec((1, rows, columns), lambda k, place: (2 * k + 1 - place[0], 0, 0)),
            ],
            out_specs=[pl.BlockSpec((width, rows), lambda k, place: (0, k))] * 4,
        ),
        out_shape=[out] * 4,
        cost_estimate=pl.CostEstimate(flops=0, bytes_accessed=4 * parts * rows * columns, transcendentals=0),
        compiler_params=pltpu.CompilerParams(vmem_limit_bytes=VMEM_LIMIT),
        name="turn",
    )(place, blocks, blocks)


def residual_kernel(pieces_ref, target_ref, out_ref):
    total = pieces_ref[0].astype(jnp.float32)
    for f in range(1, pieces_ref.shape[0]):
        total += pieces_ref[f].astype(jnp.float32)
    out_ref[...] = (total - target_ref[...].astype(jnp.float32)).astype(out_ref.dtype)


def residual_of(pieces, target):
    rows, key_width = target.shape
    parts = pieces.shape[0]
    step = rows // 4
    return pl.pallas_call(
        residual_kernel,
        grid=(4,),
        in_specs=[
            pl.BlockSpec((parts, step, key_width), lambda i: (0, i, 0)),
            pl.BlockSpec((step, key_width), lambda i: (i, 0)),
        ],
        out_specs=pl.BlockSpec((step, key_width), lambda i: (i, 0)),
        out_shape=jax.ShapeDtypeStruct((rows, key_width), jnp.bfloat16),
        compiler_params=pltpu.CompilerParams(vmem_limit_bytes=VMEM_LIMIT),
        name="residual",
    )(pieces, target)


def shards(tokens, target, weight, pseudo, global_frag, momentum):
    _, model_width = tokens.shape
    key_scale = model_width ** (-0.5)
    weight_rows = weight[0]
    _, key_width = weight_rows.shape
    place = jnp.stack([lax.axis_index("yl"), lax.axis_index("xh")]).astype(jnp.int32)

    blocks = lax.all_to_all(split_columns(tokens, lax.axis_size(Y)), Y, 0, 0, tiled=True)

    other_rows = lax.ppermute(weight_rows, "xh", SWAP)
    averaged = replica_mean(pseudo[0])

    partial = partial_keys(place, blocks, weight_rows, other_rows, key_scale)
    pieces = lax.all_to_all(partial, Y, 0, 0, tiled=True)

    send_near, keep_near, send_far, keep_far = turned(place, blocks)
    new_momentum = nesterov_coef * momentum + averaged
    new_global = global_frag - outer_rate * (averaged + nesterov_coef * new_momentum)
    merged = merge_share * weight_rows.astype(jnp.float32) + (1.0 - merge_share) * new_global
    new_momentum, new_global, merged = lax.optimization_barrier((new_momentum, new_global, merged))

    residual = residual_of(pieces, target)
    near = lax.all_gather(residual, "yh", axis=0, tiled=True)
    cut = key_width // 2
    far = []
    for c in range(2):
        far.append(lax.ppermute(near[:, c * cut : (c + 1) * cut], "yl", SWAP))

    def product(block, values):
        return jnp.dot(block, values, preferred_element_type=jnp.float32)

    sent_near = product(send_near, near)
    kept_near = merged - (merge_share * inner_rate * key_scale) * product(keep_near, near)
    sent_near, kept_near = lax.optimization_barrier((sent_near, kept_near))
    new_weight = []
    for c in range(2):
        part = slice(c * cut, (c + 1) * cut)
        sent = ((sent_near[:, part] + product(send_far, far[c])) * key_scale).astype(jnp.bfloat16)
        got = lax.ppermute(sent, "xh", SWAP)
        kept = kept_near[:, part] - (merge_share * inner_rate * key_scale) * product(keep_far, far[c])
        kept = lax.optimization_barrier(kept)
        new_weight.append((kept - (merge_share * inner_rate) * got.astype(jnp.float32)).astype(jnp.bfloat16))
    return (jnp.concatenate(new_weight, axis=1)[None], residual, new_global, new_momentum)


def solution(mesh):
    split = Mesh(mesh.devices.reshape(2, 6, 2, 2, 4, 2, 2), REPLICA + FSDP)
    rows = P(REPLICA + FSDP, None)
    per_replica = P(REPLICA, FSDP, None)
    shared = P(FSDP, None)
    return jax.shard_map(
        shards,
        mesh=split,
        in_specs=(rows, rows, per_replica, per_replica, shared, shared),
        out_specs=(per_replica, rows, shared, shared),
        check_vma=False,
    )
```

```python
import functools

import jax
import jax.numpy as jnp
from jax import lax
from jax.experimental import pallas as pl
from jax.experimental.pallas import tpu as pltpu
from jax.sharding import Mesh
from jax.sharding import PartitionSpec as P


Y = ("yh", "yl")
FSDP = ("yh", "yl", "xh")
REPLICA = ("xl", "z2", "z1", "z0", "core")
SWAP = [(0, 1), (1, 0)]
VMEM_LIMIT = 16 * 2**20

inner_rate = 1.0
outer_rate = 0.7
nesterov_coef = 0.9
merge_share = 0.5


def halved(total, axis, dim):
    me = lax.axis_index(axis)
    sent = lax.dynamic_index_in_dim(total, 1 - me, dim, keepdims=False).astype(jnp.bfloat16)
    got = lax.dynamic_index_in_dim(lax.all_gather(sent, axis), 1 - me, 0, keepdims=False)
    return lax.dynamic_index_in_dim(total, me, dim, keepdims=False) + got.astype(jnp.float32)


def replica_mean(pseudo):
    rows, columns = pseudo.shape
    replicas = lax.axis_size(REPLICA)
    total = pseudo.reshape(2, 2, 2, rows // 8, columns)
    total = halved(total, "core", 2)
    total = halved(total, "xl", 0)
    total = halved(total, "z0", 0)
    own = total.astype(jnp.bfloat16)
    other = lax.ppermute(own, "z1", SWAP)
    own = (own.astype(jnp.float32) + other.astype(jnp.float32)).astype(jnp.bfloat16)
    back1 = lax.ppermute(own, "z2", [(0, 1), (1, 2), (2, 0)])
    back2 = lax.ppermute(own, "z2", [(0, 2), (1, 0), (2, 1)])
    me = lax.axis_index("z2")

    def chosen(*values):
        return jnp.where(me == 0, values[0], jnp.where(me == 1, values[1], values[2])).astype(jnp.float32)

    summed = chosen(own, back1, back2) + chosen(back2, own, back1) + chosen(back1, back2, own)
    mean = (summed / replicas).astype(jnp.bfloat16)
    return lax.all_gather(mean, ("xl", "z0", "core"), axis=0, tiled=True).astype(jnp.float32)


def split_kernel(tokens_ref, out_ref, held, read, wrote):
    parts, _, width = held.shape

    def reading(i):
        return pltpu.make_async_copy(tokens_ref.at[:, i * width : (i + 1) * width], held.at[i], read.at[i])

    def writing(i):
        return pltpu.make_async_copy(held.at[i], out_ref.at[i], wrote.at[i])

    for i in range(parts):
        reading(i).start()
    for i in range(parts):
        reading(i).wait()
        writing(i).start()
    for i in range(parts):
        writing(i).wait()


def split_columns(tokens, parts):
    rows, columns = tokens.shape
    shape = (parts, rows, columns // parts)
    return pl.pallas_call(
        split_kernel,
        in_specs=[pl.BlockSpec(memory_space=pl.ANY)],
        out_specs=pl.BlockSpec(memory_space=pl.ANY),
        out_shape=jax.ShapeDtypeStruct(shape, tokens.dtype),
        scratch_shapes=[
            pltpu.VMEM(shape, tokens.dtype),
            pltpu.SemaphoreType.DMA((parts,)),
            pltpu.SemaphoreType.DMA((parts,)),
        ],
        name="split_columns",
    )(tokens)


def partial_kernel(scale, place_ref, x_ref, own_ref, other_ref, out_ref):
    width = own_ref.shape[0]
    rows = x_ref.shape[0] * x_ref.shape[1]
    low = x_ref[:, :, :width].reshape(rows, width)
    high = x_ref[:, :, width:].reshape(rows, width)

    def emit(low_rows, high_rows):
        total = jnp.dot(low, low_rows[...], preferred_element_type=jnp.float32)
        total += jnp.dot(high, high_rows[...], preferred_element_type=jnp.float32)
        out_ref[...] = (total * scale).astype(out_ref.dtype).reshape(out_ref.shape)

    @pl.when(place_ref[1] == 0)
    def _():
        emit(own_ref, other_ref)

    @pl.when(place_ref[1] != 0)
    def _():
        emit(other_ref, own_ref)


def partial_keys(place, blocks, own_rows, other_rows, scale):
    parts, rows, columns = blocks.shape
    width, key_width = own_rows.shape
    whole = pl.BlockSpec((width, key_width), lambda i, place: (0, 0))
    return pl.pallas_call(
        functools.partial(partial_kernel, scale),
        grid_spec=pltpu.PrefetchScalarGridSpec(
            num_scalar_prefetch=1,
            grid=(2,),
            in_specs=[pl.BlockSpec((parts // 2, rows, columns), lambda i, place: (i, 0, 0)), whole, whole],
            out_specs=pl.BlockSpec((parts // 2, rows, key_width), lambda i, place: (i, 0, 0)),
        ),
        out_shape=jax.ShapeDtypeStruct((parts, rows, key_width), jnp.bfloat16),
        cost_estimate=pl.CostEstimate(
            flops=2 * parts * rows * columns * key_width,
            bytes_accessed=2 * parts * rows * (columns + key_width) + 4 * width * key_width,
            transcendentals=0,
        ),
        compiler_params=pltpu.CompilerParams(vmem_limit_bytes=VMEM_LIMIT),
        name="partial_keys",
    )(place, blocks, own_rows, other_rows)


def turn_kernel(place_ref, near_ref, far_ref, send_near, keep_near, send_far, keep_far):
    width = send_near.shape[0]

    def emit(keep, send):
        for source, kept, sent in ((near_ref, keep_near, send_near), (far_ref, keep_far, send_far)):
            kept[...] = source[0, :, keep * width : (keep + 1) * width].T
            sent[...] = source[0, :, send * width : (send + 1) * width].T

    @pl.when(place_ref[1] == 0)
    def _():
        emit(0, 1)

    @pl.when(place_ref[1] != 0)
    def _():
        emit(1, 0)


def turned(place, blocks):
    parts, rows, columns = blocks.shape
    width = columns // 2
    out = jax.ShapeDtypeStruct((width, parts // 2 * rows), blocks.dtype)
    return pl.pallas_call(
        turn_kernel,
        grid_spec=pltpu.PrefetchScalarGridSpec(
            num_scalar_prefetch=1,
            grid=(parts // 2,),
            in_specs=[
                pl.BlockSpec((1, rows, columns), lambda k, place: (2 * k + place[0], 0, 0)),
                pl.BlockSpec((1, rows, columns), lambda k, place: (2 * k + 1 - place[0], 0, 0)),
            ],
            out_specs=[pl.BlockSpec((width, rows), lambda k, place: (0, k))] * 4,
        ),
        out_shape=[out] * 4,
        cost_estimate=pl.CostEstimate(flops=0, bytes_accessed=4 * parts * rows * columns, transcendentals=0),
        compiler_params=pltpu.CompilerParams(vmem_limit_bytes=56 * 2**20),
        name="turn",
    )(place, blocks, blocks)


def residual_kernel(pieces_ref, target_ref, out_ref):
    total = pieces_ref[0].astype(jnp.float32)
    for f in range(1, pieces_ref.shape[0]):
        total += pieces_ref[f].astype(jnp.float32)
    out_ref[...] = (total - target_ref[...].astype(jnp.float32)).astype(out_ref.dtype)


def residual_of(pieces, target):
    rows, key_width = target.shape
    parts = pieces.shape[0]
    step = rows // 4
    return pl.pallas_call(
        residual_kernel,
        grid=(4,),
        in_specs=[
            pl.BlockSpec((parts, step, key_width), lambda i: (0, i, 0)),
            pl.BlockSpec((step, key_width), lambda i: (i, 0)),
        ],
        out_specs=pl.BlockSpec((step, key_width), lambda i: (i, 0)),
        out_shape=jax.ShapeDtypeStruct((rows, key_width), jnp.bfloat16),
        compiler_params=pltpu.CompilerParams(vmem_limit_bytes=VMEM_LIMIT),
        name="residual",
    )(pieces, target)


def shards(tokens, target, weight, pseudo, global_frag, momentum):
    _, model_width = tokens.shape
    key_scale = model_width ** (-0.5)
    weight_rows = weight[0]
    _, key_width = weight_rows.shape
    place = jnp.stack([lax.axis_index("yl"), lax.axis_index("xh")]).astype(jnp.int32)

    blocks = lax.all_to_all(split_columns(tokens, lax.axis_size(Y)), Y, 0, 0, tiled=True)

    other_rows = lax.ppermute(weight_rows, "xh", SWAP)
    averaged = replica_mean(pseudo[0])

    partial = partial_keys(place, blocks, weight_rows, other_rows, key_scale)
    pieces = lax.all_to_all(partial, Y, 0, 0, tiled=True)

    send_near, keep_near, send_far, keep_far = turned(place, blocks)
    residual = residual_of(pieces, target)
    near = lax.all_gather(residual, "yh", axis=0, tiled=True)
    cut = key_width // 2
    far = []
    for c in range(2):
        far.append(lax.ppermute(near[:, c * cut : (c + 1) * cut], "yl", SWAP))

    def product(block, values):
        return jnp.dot(block, values, preferred_element_type=jnp.float32)

    sent_near = product(send_near, near)
    kept_near = product(keep_near, near)
    got = []
    for c in range(2):
        part = slice(c * cut, (c + 1) * cut)
        sent = ((sent_near[:, part] + product(send_far, far[c])) * key_scale).astype(jnp.bfloat16)
        got.append(lax.ppermute(sent, "xh", SWAP))

    averaged, _ = lax.optimization_barrier((averaged, sent))
    new_momentum = nesterov_coef * momentum + averaged
    new_global = global_frag - outer_rate * (averaged + nesterov_coef * new_momentum)
    merged = merge_share * weight_rows.astype(jnp.float32) + (1.0 - merge_share) * new_global
    new_weight = []
    for c in range(2):
        part = slice(c * cut, (c + 1) * cut)
        gradient = (kept_near[:, part] + product(keep_far, far[c])) * key_scale
        kept = lax.optimization_barrier(merged[:, part] - (merge_share * inner_rate) * gradient)
        new_weight.append((kept - (merge_share * inner_rate) * got[c].astype(jnp.float32)).astype(jnp.bfloat16))
    return (jnp.concatenate(new_weight, axis=1)[None], residual, new_global, new_momentum)


def solution(mesh):
    split = Mesh(mesh.devices.reshape(2, 3, 2, 2, 2, 4, 2, 2), REPLICA + FSDP)
    rows = P(REPLICA + FSDP, None)
    per_replica = P(REPLICA, FSDP, None)
    shared = P(FSDP, None)
    return jax.shard_map(
        shards,
        mesh=split,
        in_specs=(rows, rows, per_replica, per_replica, shared, shared),
        out_specs=(per_replica, rows, shared, shared),
        check_vma=False,
    )
```

```python
import functools

import jax
import jax.numpy as jnp
from jax import lax
from jax.experimental import pallas as pl
from jax.experimental.pallas import tpu as pltpu
from jax.sharding import Mesh
from jax.sharding import PartitionSpec as P


Y = ("yl", "yh")
FSDP = ("yh", "yl", "xh")
REPLICA = ("xl", "z2", "z1", "z0", "core")
SWAP = [(0, 1), (1, 0)]
VMEM_LIMIT = 16 * 2**20

inner_rate = 1.0
outer_rate = 0.7
nesterov_coef = 0.9
merge_share = 0.5


def halved(total, axis, dim):
    me = lax.axis_index(axis)
    sent = lax.dynamic_index_in_dim(total, 1 - me, dim, keepdims=False).astype(jnp.bfloat16)
    got = lax.dynamic_index_in_dim(lax.all_gather(sent, axis), 1 - me, 0, keepdims=False)
    return lax.dynamic_index_in_dim(total, me, dim, keepdims=False) + got.astype(jnp.float32)


def replica_mean(pseudo):
    rows, columns = pseudo.shape
    replicas = lax.axis_size(REPLICA)
    total = pseudo.reshape(2, 2, 2, rows // 8, columns)
    total = halved(total, "core", 2)
    total = halved(total, "xl", 0)
    total = halved(total, "z0", 0)
    own = total.astype(jnp.bfloat16)
    other = lax.ppermute(own, "z1", SWAP)
    own = (own.astype(jnp.float32) + other.astype(jnp.float32)).astype(jnp.bfloat16)
    back1 = lax.ppermute(own, "z2", [(0, 1), (1, 2), (2, 0)])
    back2 = lax.ppermute(own, "z2", [(0, 2), (1, 0), (2, 1)])
    me = lax.axis_index("z2")

    def chosen(*values):
        return jnp.where(me == 0, values[0], jnp.where(me == 1, values[1], values[2])).astype(jnp.float32)

    summed = chosen(own, back1, back2) + chosen(back2, own, back1) + chosen(back1, back2, own)
    mean = (summed / replicas).astype(jnp.bfloat16)
    return lax.all_gather(mean, ("xl", "z0", "core"), axis=0, tiled=True).astype(jnp.float32)


def split_kernel(tokens_ref, out_ref, held, read, wrote):
    parts, _, width = held.shape

    def reading(i):
        return pltpu.make_async_copy(tokens_ref.at[:, i * width : (i + 1) * width], held.at[i], read.at[i])

    def writing(i):
        place = i % 2 * (parts // 2) + i // 2
        return pltpu.make_async_copy(held.at[i], out_ref.at[place], wrote.at[i])

    for i in range(parts):
        reading(i).start()
    for i in range(parts):
        reading(i).wait()
        writing(i).start()
    for i in range(parts):
        writing(i).wait()


def split_columns(tokens, parts):
    rows, columns = tokens.shape
    shape = (parts, rows, columns // parts)
    return pl.pallas_call(
        split_kernel,
        in_specs=[pl.BlockSpec(memory_space=pl.ANY)],
        out_specs=pl.BlockSpec(memory_space=pl.ANY),
        out_shape=jax.ShapeDtypeStruct(shape, tokens.dtype),
        scratch_shapes=[
            pltpu.VMEM(shape, tokens.dtype),
            pltpu.SemaphoreType.DMA((parts,)),
            pltpu.SemaphoreType.DMA((parts,)),
        ],
        name="split_columns",
    )(tokens)


def partial_kernel(scale, x_ref, rows_ref, out_ref):
    parts, rows, columns = x_ref.shape
    total = jnp.dot(
        x_ref[...].reshape(parts * rows, columns), rows_ref[...], preferred_element_type=jnp.float32
    )
    out_ref[...] = (total * scale).astype(out_ref.dtype).reshape(out_ref.shape)


def partial_keys(blocks, weight_rows, scale):
    parts, rows, columns = blocks.shape
    key_width = weight_rows.shape[1]
    return pl.pallas_call(
        functools.partial(partial_kernel, scale),
        grid=(2,),
        in_specs=[
            pl.BlockSpec((parts // 2, rows, columns), lambda i: (i, 0, 0)),
            pl.BlockSpec((columns, key_width), lambda i: (0, 0)),
        ],
        out_specs=pl.BlockSpec((parts // 2, rows, key_width), lambda i: (i, 0, 0)),
        out_shape=pltpu.HBM((parts, rows, key_width), jnp.bfloat16),
        compiler_params=pltpu.CompilerParams(vmem_limit_bytes=VMEM_LIMIT),
        cost_estimate=pl.CostEstimate(
            flops=2 * parts * rows * columns * key_width,
            bytes_accessed=2 * parts * rows * (columns + key_width) + 2 * columns * key_width,
            transcendentals=0,
        ),
        name="partial_keys",
    )(blocks, weight_rows)


def turn_kernel(place_ref, near_ref, far_ref, send_near, keep_near, send_far, keep_far):
    width = send_near.shape[0]

    def emit(keep, send):
        for source, kept, sent in ((near_ref, keep_near, send_near), (far_ref, keep_far, send_far)):
            kept[...] = source[0, :, keep * width : (keep + 1) * width].T
            sent[...] = source[0, :, send * width : (send + 1) * width].T

    @pl.when(place_ref[1] == 0)
    def _():
        emit(0, 1)

    @pl.when(place_ref[1] != 0)
    def _():
        emit(1, 0)


def turned(place, blocks):
    parts, rows, columns = blocks.shape
    width = columns // 2
    out = pltpu.HBM((width, parts // 2 * rows), blocks.dtype)
    return pl.pallas_call(
        turn_kernel,
        grid_spec=pltpu.PrefetchScalarGridSpec(
            num_scalar_prefetch=1,
            grid=(parts // 2,),
            in_specs=[
                pl.BlockSpec((1, rows, columns), lambda k, place: (4 * place[0] + k, 0, 0)),
                pl.BlockSpec((1, rows, columns), lambda k, place: (4 - 4 * place[0] + k, 0, 0)),
            ],
            out_specs=[pl.BlockSpec((width, rows), lambda k, place: (0, k))] * 4,
        ),
        out_shape=[out] * 4,
        cost_estimate=pl.CostEstimate(flops=0, bytes_accessed=4 * parts * rows * columns, transcendentals=0),
        compiler_params=pltpu.CompilerParams(vmem_limit_bytes=VMEM_LIMIT),
        name="turn",
    )(place, blocks, blocks)


def residual_kernel(pieces_ref, target_ref, out_ref):
    step = 16

    def rows_of(i, _):
        rows = pl.ds(pl.multiple_of(i * step, step), step)
        total = pieces_ref[0, rows, :].astype(jnp.float32)
        for f in range(1, pieces_ref.shape[0]):
            total += pieces_ref[f, rows, :].astype(jnp.float32)
        out_ref[rows, :] = (total - target_ref[rows, :].astype(jnp.float32)).astype(out_ref.dtype)
        return _

    lax.fori_loop(0, out_ref.shape[0] // step, rows_of, 0, unroll=True)


def residual_of(pieces, target):
    vmem = pl.BlockSpec(memory_space=pltpu.VMEM)
    return pl.pallas_call(
        residual_kernel,
        in_specs=[vmem, vmem],
        out_specs=vmem,
        out_shape=jax.ShapeDtypeStruct(target.shape, jnp.bfloat16),
        compiler_params=pltpu.CompilerParams(vmem_limit_bytes=VMEM_LIMIT),
        name="residual",
    )(pieces, target)


def shards(tokens, target, weight, pseudo, global_frag, momentum):
    own_tokens, model_width = tokens.shape
    key_scale = model_width ** (-0.5)
    weight_rows = weight[0]
    width, key_width = weight_rows.shape
    place = jnp.stack([lax.axis_index("yl"), lax.axis_index("xh")]).astype(jnp.int32)

    blocks = lax.all_to_all(split_columns(tokens, lax.axis_size(Y)), Y, 0, 0, tiled=True)

    other_rows = lax.ppermute(weight_rows, "xh", SWAP)
    first = lax.axis_index("xh") == 0
    both_rows = jnp.concatenate(
        [jnp.where(first, weight_rows, other_rows), jnp.where(first, other_rows, weight_rows)], axis=0
    )
    averaged = replica_mean(pseudo[0])

    partial = partial_keys(blocks, both_rows, key_scale)
    pieces = lax.all_to_all(partial, Y, 0, 0, tiled=True)

    send_near, keep_near, send_far, keep_far = turned(place, blocks)
    residual = residual_of(pieces, target)
    near = lax.all_gather(residual, "yh", axis=0, tiled=True)
    cut = key_width // 2
    far = []
    for c in range(2):
        far.append(lax.ppermute(near[:, c * cut : (c + 1) * cut], "yl", SWAP))

    def product(block, values):
        return jnp.dot(block, values, preferred_element_type=jnp.float32)

    sent_near = product(send_near, near)
    kept_near = product(keep_near, near)
    got = []
    for c in range(2):
        part = slice(c * cut, (c + 1) * cut)
        sent = ((sent_near[:, part] + product(send_far, far[c])) * key_scale).astype(jnp.bfloat16)
        got.append(lax.ppermute(sent, "xh", SWAP))

    averaged, _ = lax.optimization_barrier((averaged, sent))
    new_momentum = nesterov_coef * momentum + averaged
    new_global = global_frag - outer_rate * (averaged + nesterov_coef * new_momentum)
    merged = merge_share * weight_rows.astype(jnp.float32) + (1.0 - merge_share) * new_global
    new_weight = []
    for c in range(2):
        part = slice(c * cut, (c + 1) * cut)
        gradient = (kept_near[:, part] + product(keep_far, far[c])) * key_scale
        kept = lax.optimization_barrier(merged[:, part] - (merge_share * inner_rate) * gradient)
        new_weight.append((kept - (merge_share * inner_rate) * got[c].astype(jnp.float32)).astype(jnp.bfloat16))
    return (jnp.concatenate(new_weight, axis=1)[None], residual, new_global, new_momentum)


def solution(mesh):
    split = Mesh(mesh.devices.reshape(2, 3, 2, 2, 2, 4, 2, 2), REPLICA + FSDP)
    rows = P(REPLICA + FSDP, None)
    per_replica = P(REPLICA, FSDP, None)
    shared = P(FSDP, None)
    return jax.shard_map(
        shards,
        mesh=split,
        in_specs=(rows, rows, per_replica, per_replica, shared, shared),
        out_specs=(per_replica, rows, shared, shared),
        check_vma=False,
    )
```

```python
import functools

import jax
import jax.numpy as jnp
from jax import lax
from jax.experimental import pallas as pl
from jax.experimental.pallas import tpu as pltpu
from jax.sharding import Mesh
from jax.sharding import PartitionSpec as P


Y = ("yl", "yh")
FSDP = ("yh", "yl", "xh")
REPLICA = ("xl", "z2", "z1", "z0", "core")
SWAP = [(0, 1), (1, 0)]
VMEM_LIMIT = 16 * 2**20

inner_rate = 1.0
outer_rate = 0.7
nesterov_coef = 0.9
merge_share = 0.5


def halved(total, axis, dim):
    me = lax.axis_index(axis)
    sent = lax.dynamic_index_in_dim(total, 1 - me, dim, keepdims=False).astype(jnp.bfloat16)
    got = lax.dynamic_index_in_dim(lax.all_gather(sent, axis), 1 - me, 0, keepdims=False)
    return lax.dynamic_index_in_dim(total, me, dim, keepdims=False) + got.astype(jnp.float32)


def replica_mean(pseudo):
    rows, columns = pseudo.shape
    replicas = lax.axis_size(REPLICA)
    total = pseudo.reshape(2, 2, 2, rows // 8, columns)
    total = halved(total, "core", 2)
    total = halved(total, "xl", 0)
    total = halved(total, "z0", 0)
    own = total.astype(jnp.bfloat16)
    other = lax.ppermute(own, "z1", SWAP)
    own = (own.astype(jnp.float32) + other.astype(jnp.float32)).astype(jnp.bfloat16)
    back1 = lax.ppermute(own, "z2", [(0, 1), (1, 2), (2, 0)])
    back2 = lax.ppermute(own, "z2", [(0, 2), (1, 0), (2, 1)])
    me = lax.axis_index("z2")

    def chosen(*values):
        return jnp.where(me == 0, values[0], jnp.where(me == 1, values[1], values[2])).astype(jnp.float32)

    summed = chosen(own, back1, back2) + chosen(back2, own, back1) + chosen(back1, back2, own)
    mean = (summed / replicas).astype(jnp.bfloat16)
    return lax.all_gather(mean, ("xl", "z0", "core"), axis=0, tiled=True).astype(jnp.float32)


def split_kernel(tokens_ref, out_ref, held, read, wrote):
    parts, _, width = held.shape

    def reading(i):
        return pltpu.make_async_copy(tokens_ref.at[:, i * width : (i + 1) * width], held.at[i], read.at[i])

    def writing(i):
        place = i % 2 * (parts // 2) + i // 2
        return pltpu.make_async_copy(held.at[i], out_ref.at[place], wrote.at[i])

    for i in range(parts):
        reading(i).start()
    for i in range(parts):
        reading(i).wait()
        writing(i).start()
    for i in range(parts):
        writing(i).wait()


def split_columns(tokens, parts):
    rows, columns = tokens.shape
    shape = (parts, rows, columns // parts)
    return pl.pallas_call(
        split_kernel,
        in_specs=[pl.BlockSpec(memory_space=pl.ANY)],
        out_specs=pl.BlockSpec(memory_space=pl.ANY),
        out_shape=jax.ShapeDtypeStruct(shape, tokens.dtype),
        scratch_shapes=[
            pltpu.VMEM(shape, tokens.dtype),
            pltpu.SemaphoreType.DMA((parts,)),
            pltpu.SemaphoreType.DMA((parts,)),
        ],
        name="split_columns",
    )(tokens)


def partial_kernel(scale, x_ref, rows_ref, out_ref):
    parts, rows, _ = out_ref.shape
    block = x_ref[pl.ds(pl.program_id(0) * parts, parts)]
    total = jnp.dot(
        block.reshape(parts * rows, x_ref.shape[2]), rows_ref[...], preferred_element_type=jnp.float32
    )
    out_ref[...] = (total * scale).astype(out_ref.dtype).reshape(out_ref.shape)


def partial_keys(blocks, weight_rows, scale):
    parts, rows, columns = blocks.shape
    key_width = weight_rows.shape[1]
    return pl.pallas_call(
        functools.partial(partial_kernel, scale),
        grid=(2,),
        in_specs=[pl.BlockSpec(memory_space=pltpu.VMEM)] * 2,
        out_specs=pl.BlockSpec((parts // 2, rows, key_width), lambda i: (i, 0, 0)),
        out_shape=pltpu.HBM((parts, rows, key_width), jnp.bfloat16),
        compiler_params=pltpu.CompilerParams(vmem_limit_bytes=VMEM_LIMIT),
        cost_estimate=pl.CostEstimate(
            flops=2 * parts * rows * columns * key_width,
            bytes_accessed=2 * parts * rows * (columns + key_width) + 2 * columns * key_width,
            transcendentals=0,
        ),
        name="partial_keys",
    )(blocks, weight_rows)


def turn_kernel(place_ref, near_ref, far_ref, send_near, keep_near, send_far, keep_far):
    width = send_near.shape[0]

    def emit(keep, send):
        for source, kept, sent in ((near_ref, keep_near, send_near), (far_ref, keep_far, send_far)):
            kept[...] = source[0, :, keep * width : (keep + 1) * width].T
            sent[...] = source[0, :, send * width : (send + 1) * width].T

    @pl.when(place_ref[1] == 0)
    def _():
        emit(0, 1)

    @pl.when(place_ref[1] != 0)
    def _():
        emit(1, 0)


def turned(place, blocks):
    parts, rows, columns = blocks.shape
    width = columns // 2
    out = pltpu.HBM((width, parts // 2 * rows), blocks.dtype)
    return pl.pallas_call(
        turn_kernel,
        grid_spec=pltpu.PrefetchScalarGridSpec(
            num_scalar_prefetch=1,
            grid=(parts // 2,),
            in_specs=[
                pl.BlockSpec((1, rows, columns), lambda k, place: (4 * place[0] + k, 0, 0)),
                pl.BlockSpec((1, rows, columns), lambda k, place: (4 - 4 * place[0] + k, 0, 0)),
            ],
            out_specs=[pl.BlockSpec((width, rows), lambda k, place: (0, k))] * 4,
        ),
        out_shape=[out] * 4,
        cost_estimate=pl.CostEstimate(flops=0, bytes_accessed=4 * parts * rows * columns, transcendentals=0),
        compiler_params=pltpu.CompilerParams(vmem_limit_bytes=VMEM_LIMIT),
        name="turn",
    )(place, blocks, blocks)


def residual_kernel(pieces_ref, target_ref, out_ref):
    step = 16

    def rows_of(i, _):
        rows = pl.ds(pl.multiple_of(i * step, step), step)
        total = pieces_ref[0, rows, :].astype(jnp.float32)
        for f in range(1, pieces_ref.shape[0]):
            total += pieces_ref[f, rows, :].astype(jnp.float32)
        out_ref[rows, :] = (total - target_ref[rows, :].astype(jnp.float32)).astype(out_ref.dtype)
        return _

    lax.fori_loop(0, out_ref.shape[0] // step, rows_of, 0, unroll=True)


def residual_of(pieces, target):
    vmem = pl.BlockSpec(memory_space=pltpu.VMEM)
    return pl.pallas_call(
        residual_kernel,
        in_specs=[vmem, vmem],
        out_specs=vmem,
        out_shape=jax.ShapeDtypeStruct(target.shape, jnp.bfloat16),
        compiler_params=pltpu.CompilerParams(vmem_limit_bytes=VMEM_LIMIT),
        name="residual",
    )(pieces, target)


def shards(tokens, target, weight, pseudo, global_frag, momentum):
    own_tokens, model_width = tokens.shape
    key_scale = model_width ** (-0.5)
    weight_rows = weight[0]
    width, key_width = weight_rows.shape
    place = jnp.stack([lax.axis_index("yl"), lax.axis_index("xh")]).astype(jnp.int32)

    blocks = lax.all_to_all(split_columns(tokens, lax.axis_size(Y)), Y, 0, 0, tiled=True)

    other_rows = lax.ppermute(weight_rows, "xh", SWAP)
    first = lax.axis_index("xh") == 0
    both_rows = jnp.concatenate(
        [jnp.where(first, weight_rows, other_rows), jnp.where(first, other_rows, weight_rows)], axis=0
    )
    averaged = replica_mean(pseudo[0])

    partial = partial_keys(blocks, both_rows, key_scale)
    pieces = lax.all_to_all(partial, Y, 0, 0, tiled=True)

    send_near, keep_near, send_far, keep_far = turned(place, blocks)
    residual = residual_of(pieces, target)
    near = lax.all_gather(residual, "yh", axis=0, tiled=True)
    cut = key_width // 2
    far = []
    for c in range(2):
        far.append(lax.ppermute(near[:, c * cut : (c + 1) * cut], "yl", SWAP))

    def product(block, values):
        return jnp.dot(block, values, preferred_element_type=jnp.float32)

    sent_near = product(send_near, near)
    kept_near = product(keep_near, near)
    got = []
    for c in range(2):
        part = slice(c * cut, (c + 1) * cut)
        sent = ((sent_near[:, part] + product(send_far, far[c])) * key_scale).astype(jnp.bfloat16)
        got.append(lax.ppermute(sent, "xh", SWAP))

    averaged, _ = lax.optimization_barrier((averaged, sent))
    new_momentum = nesterov_coef * momentum + averaged
    new_global = global_frag - outer_rate * (averaged + nesterov_coef * new_momentum)
    merged = merge_share * weight_rows.astype(jnp.float32) + (1.0 - merge_share) * new_global
    new_weight = []
    for c in range(2):
        part = slice(c * cut, (c + 1) * cut)
        gradient = (kept_near[:, part] + product(keep_far, far[c])) * key_scale
        kept = lax.optimization_barrier(merged[:, part] - (merge_share * inner_rate) * gradient)
        new_weight.append((kept - (merge_share * inner_rate) * got[c].astype(jnp.float32)).astype(jnp.bfloat16))
    return (jnp.concatenate(new_weight, axis=1)[None], residual, new_global, new_momentum)


def solution(mesh):
    split = Mesh(mesh.devices.reshape(2, 3, 2, 2, 2, 4, 2, 2), REPLICA + FSDP)
    rows = P(REPLICA + FSDP, None)
    per_replica = P(REPLICA, FSDP, None)
    shared = P(FSDP, None)
    return jax.shard_map(
        shards,
        mesh=split,
        in_specs=(rows, rows, per_replica, per_replica, shared, shared),
        out_specs=(per_replica, rows, shared, shared),
        check_vma=False,
    )
```
